128 devices in a mesh: tm: 4 (over x), slab: 32 (over z, y, core).
Axes of the slice: x: 4, y: 4, z: 4, core: 2. Of those that a mesh axis runs over, the one named last changes fastest.
Arguments:
- eigvecs: float32 [4, 3, 13824, 2, 128], P('tm', None, 'slab'), may hold values from -6 to 6
- perambulator: float32 [512, 8, 2, 512], P('slab', 'tm'), may hold values from -0.015625 to 0.015625
- time_pairs: int32 [8, 2], P('tm'), may hold values from 0 to 3
- momenta: int32 [4, 3], replicated, may hold values from -2 to 2, as said below
Outputs:
- dressed: float32 [512, 8, 4, 2, 512], P('slab', 'tm')
The draws below stay inside these ranges and needn't reach their ends.
Inputs may be any that keep to these rules, and one draw needn't show every extreme that they name: `momenta`: every component of each momentum is nonzero.
All inputs are finite; a program needn't handle non-finite values.
Results may differ from the reference program's by a relative error of at most 0.0001.
Values sent between devices are 32-bit elements; how exact they have to be, the bound alone decides.
No kernel may reach another device: no remote copies, remote signals or barrier semaphores. Data moves between devices by JAX's collectives and lax.ppermute only.
A program may use at most 64 MiB of HBM per device.

```python
import math
import jax
import jax.numpy as jnp
from jax import lax

NVEC = 128
NCOL = 3
LS = 48
NMOM = 4
NS = 512
NT = 4
NSITE = 13824
NPAIR = 8


def draw_momenta(key, part):
    magnitude = jax.random.randint(jax.random.fold_in(key, 11), (NMOM, 3), 1, 3)
    flips = jax.random.randint(jax.random.fold_in(key, 12), (NMOM, 3), 0, 2) * 2 - 1
    return (magnitude * flips).astype(jnp.int32)


def with_ends(result, key, least, high):
    extent = result.shape
    place = [jax.random.randint(jax.random.fold_in(key, axis), (), 0, extent[axis]) for axis in range(len(extent))]
    result = result.at[tuple(place)].set(least)
    longest = extent.index(max(extent))
    place[longest] = (place[longest] + 1) % extent[longest]
    return result.at[tuple(place)].set(high)


def shard_levels(key, dims, cuts, least, top_value):
    level = 1.0
    for position, parts in cuts:
        draws = jax.random.uniform(jax.random.fold_in(jax.random.fold_in(key, 6), position), (parts,), jnp.float32, least / len(cuts), top_value / len(cuts))
        level = level * jnp.repeat(jnp.exp(draws), dims[position] // parts).reshape((-1,) + (1,) * (len(dims) - 1 - position))
    return level


def noise(rng, shape, scale, limit, split=(), held_as=jnp.bfloat16):
    result = jax.random.normal(rng, shape, jnp.float32) * scale
    if len(split) > 0:
        result = shard_levels(rng, shape, split, -0.22, 0.18) * result
    return jnp.clip(result, min=-limit, max=limit).astype(held_as)


def setup_inputs(seed: int = 0) -> dict:
    key_of = jax.random.split(jax.random.key(seed), 5)
    eigvecs = noise(key_of[0], (NT, NCOL, NSITE, 2, NVEC), 1.0, 6.0, ((0, 4), (2, 32)), jnp.float32)
    perambulator = noise(key_of[1], (NS, NPAIR, 2, NS), (NS * NS // 2) ** -0.5, 0.015625, ((0, 32), (1, 4)), jnp.float32)
    time_pairs = with_ends(jax.random.randint(key_of[2], (NPAIR, 2), 0, NT), jax.random.fold_in(key_of[2], 1), 0, NT - 1).astype(jnp.int32)
    momenta = draw_momenta(jax.random.fold_in(key_of[4], 71), 0)
    return {"eigvecs": eigvecs, "perambulator": perambulator, "time_pairs": time_pairs, "momenta": momenta}


PRECISE = lax.Precision.HIGHEST
SPIN_MIX = ((1.0, 0.0, 1.0, 0.0), (0.0, 1.0, 0.0, 1.0), (1.0, 0.0, 1.0, 0.0), (0.0, 1.0, 0.0, 1.0))
CHIRAL = (1.0, 1.0, -1.0, -1.0)

def spin_tables():
    spin_mix = jnp.array(SPIN_MIX, jnp.float32)
    chiral = jnp.array(CHIRAL, jnp.float32)
    spin_dressed = chiral[:, None] * spin_mix * chiral[None, :]
    return (spin_mix, spin_dressed)

def phase_tables(momenta, site_ids):
    coords = jnp.stack([site_ids % LS, site_ids // LS % LS, site_ids // (LS * LS)])
    phase_turns = jnp.mod(lax.optimization_barrier(jnp.sum(momenta[:, :, None] * coords[None, :, :], axis=1)), LS)
    phase_angle = phase_turns.astype(jnp.float32) * (2.0 * math.pi / LS)
    return (jnp.cos(phase_angle), jnp.sin(phase_angle))

def elemental_terms(vectors, cosine_tab, sine_tab):
    local_times = vectors.shape[0]
    vec_count = vectors.shape[4]
    real_part = vectors[:, :, :, 0, :]
    imag_part = vectors[:, :, :, 1, :]
    left_rows = vectors.reshape(local_times, -1, vec_count)
    per_moment = []
    for mom_index in range(cosine_tab.shape[0]):
        cos_here = cosine_tab[mom_index][None, None, :, None]
        sin_here = sine_tab[mom_index][None, None, :, None]
        turned_re = cos_here * real_part - sin_here * imag_part
        turned_im = sin_here * real_part + cos_here * imag_part
        first_half = jnp.stack([turned_re, turned_im], axis=3).reshape(local_times, -1, vec_count)
        second_half = jnp.stack([turned_im, -turned_re], axis=3).reshape(local_times, -1, vec_count)
        right_cols = jnp.concatenate([first_half, second_half], axis=2)
        product = jnp.einsum('tki,tkj->tij', left_rows, right_cols, precision=PRECISE)
        per_moment.append(product.reshape(local_times, vec_count, 2, vec_count).transpose(0, 2, 1, 3))
    return jnp.stack(per_moment, axis=1)

def plain_dot(left_mat, right_mat):
    return jnp.dot(left_mat, right_mat, precision=PRECISE, preferred_element_type=jnp.float32)

def complex_dot(left_re, left_im, right_re, right_im):
    return (plain_dot(left_re, right_re) - plain_dot(left_im, right_im), plain_dot(left_re, right_im) + plain_dot(left_im, right_re))

def reference(eigvecs, perambulator, time_pairs, momenta):
    site_ids = jnp.arange(NSITE, dtype=jnp.int32)
    cosine_tab, sine_tab = phase_tables(momenta, site_ids)
    elementals = lax.map(lambda slice_vec: elemental_terms(slice_vec[None], cosine_tab, sine_tab)[0], eigvecs)
    elementals = elementals * (1.0 / math.sqrt(2.0 * NCOL * NSITE))
    spin_mix, spin_dressed = spin_tables()

    def dress_pair(index_pair):
        sink_elem = elementals[time_pairs[index_pair, 1]]
        source_elem = elementals[time_pairs[index_pair, 0]]
        peram_pair = lax.dynamic_index_in_dim(perambulator, index_pair, 1, keepdims=False)
        peram_re = peram_pair[:, 0, :].T
        peram_im = peram_pair[:, 1, :].T
        per_moment = []
        for mom_index in range(NMOM):
            outer_re = jnp.kron(spin_mix, sink_elem[mom_index, 0])
            outer_im = jnp.kron(spin_mix, sink_elem[mom_index, 1])
            dress_re = jnp.kron(spin_dressed, source_elem[mom_index, 0].T)
            dress_im = -jnp.kron(spin_dressed, source_elem[mom_index, 1].T)
            inner_re, inner_im = complex_dot(outer_re, outer_im, peram_re, peram_im)
            final_re, final_im = complex_dot(inner_re, inner_im, dress_re, dress_im)
            per_moment.append(jnp.stack([final_re.T, final_im.T], axis=1))
        return jnp.stack(per_moment, axis=1)
    stacked = lax.map(dress_pair, jnp.arange(NPAIR, dtype=jnp.int32))
    return jnp.transpose(stacked, (1, 0, 2, 3, 4))
```

```python
import math

import jax
import jax.numpy as jnp
from jax import lax
from jax.experimental import pallas as pl
from jax.experimental.pallas import tpu as pltpu
from jax.sharding import Mesh
from jax.sharding import PartitionSpec as P

LS = 48
NMOM = 4
NVEC = 128
NCOL = 3
SITES = 432
ROWS = NCOL * SITES
NSITE = 13824
BLK = 16
F32 = jnp.float32
BF16 = jnp.bfloat16
INTERPRET = False


def halves(x):
    hi = x.astype(BF16)
    return hi, (x - hi.astype(F32)).astype(BF16)


def dot(a, b):
    return jnp.dot(a, b, preferred_element_type=F32)


def over48(x):
    return lax.shift_right_logical(x * 43691, 21)


def phase_rows(mom, slab):
    lane = lax.broadcasted_iota(jnp.int32, (8, ROWS), 1)
    row = lax.broadcasted_iota(jnp.int32, (8, ROWS), 0)
    site = lane - jnp.where(lane >= 2 * SITES, 2 * SITES, jnp.where(lane >= SITES, SITES, 0)) + slab * SITES
    line = over48(site)
    plane = over48(line)
    coords = (site - LS * line, line - LS * plane, plane)
    mrow = row & 3
    turns = jnp.where(row >= 4, 7 * LS - 12, 6 * LS)
    for d in range(3):
        p = jnp.where(mrow == 0, mom[0, d], jnp.where(mrow == 1, mom[1, d], jnp.where(mrow == 2, mom[2, d], mom[3, d])))
        turns = turns + p * coords[d]
    turns = turns - LS * over48(turns)
    return jnp.cos(turns.astype(F32) * (2.0 * math.pi / LS))


def elemental_kernel(mom, slab, x, o, at, bt, whi, wlo, uhi, ulo):
    tab = phase_rows(mom, slab[0])
    a = x[pl.ds(0, ROWS, stride=2), :]
    b = x[pl.ds(1, ROWS, stride=2), :]
    for n, v in enumerate((a, b)):
        hi, lo = halves(v)
        whi[:, n * NVEC:(n + 1) * NVEC] = hi
        wlo[:, n * NVEC:(n + 1) * NVEC] = lo
    at[...] = a.T
    bt[...] = b.T
    for m in range(NMOM):
        for k0 in range(0, ROWS, 128):
            ks = slice(k0, min(k0 + 128, ROWS))
            cos, sin = tab[m:m + 1, ks], tab[4 + m:5 + m, ks]
            ak, bk = at[:, ks], bt[:, ks]
            for n, u in enumerate((cos * ak + sin * bk, cos * bk - sin * ak)):
                hi, lo = halves(u)
                uhi[m, n * NVEC:(n + 1) * NVEC, ks] = hi
                ulo[m, n * NVEC:(n + 1) * NVEC, ks] = lo
        prod = dot(uhi[m], whi[...]) + dot(ulo[m], whi[...]) + dot(uhi[m], wlo[...])
        re = prod[:NVEC, :NVEC] + prod[NVEC:, NVEC:]
        im = prod[:NVEC, NVEC:] - prod[NVEC:, :NVEC]
        o[m, :, 0] = re.reshape(8, BLK, NVEC)
        o[m, :, 1] = im.reshape(8, BLK, NVEC)


def elementals(mom, slab, x):
    return pl.pallas_call(
        elemental_kernel,
        out_shape=jax.ShapeDtypeStruct((NMOM, 8, 2, BLK, NVEC), F32),
        in_specs=[
            pl.BlockSpec(memory_space=pltpu.SMEM),
            pl.BlockSpec(memory_space=pltpu.SMEM),
            pl.BlockSpec(memory_space=pltpu.VMEM),
        ],
        out_specs=pl.BlockSpec(memory_space=pltpu.VMEM),
        scratch_shapes=[
            pltpu.VMEM((NVEC, ROWS), F32),
            pltpu.VMEM((NVEC, ROWS), F32),
            pltpu.VMEM((ROWS, 2 * NVEC), BF16),
            pltpu.VMEM((ROWS, 2 * NVEC), BF16),
            pltpu.VMEM((NMOM, 2 * NVEC, ROWS), BF16),
            pltpu.VMEM((NMOM, 2 * NVEC, ROWS), BF16),
        ],
        name="elementals",
        interpret=INTERPRET,
    )(mom, slab, x)


def times_i(x):
    rows = x.shape[0]
    y = x.reshape(rows // 8, 8, x.shape[1])
    even = lax.broadcasted_iota(jnp.int32, y.shape, 1) % 2 == 0
    y = jnp.where(even, -pltpu.roll(y, 7, 1), pltpu.roll(y, 1, 1))
    return y.reshape(x.shape)


def dress_kernel(tp, place, e, r, keep, send, lrows):
    y, c = place[0], place[1]
    t1, t2 = tp[c, 0], tp[c, 1]
    sink = e[t2]
    cat = jnp.concatenate([sink[:, 0].reshape(NVEC, NVEC), sink[:, 1].reshape(NVEC, NVEC)], axis=1)
    ehi, elo = halves(cat)
    e_both = jnp.concatenate([ehi, elo], axis=0)
    for n in range(2):
        blk = 2 * y + (c if n == 0 else 1 - c)
        src = e[t1, blk]
        lrows[pl.ds(2 * BLK * n, BLK, stride=2), :] = src[0]
        lrows[pl.ds(2 * BLK * n + 1, BLK, stride=2), :] = -src[1]
    left = lrows[...]
    lhi, llo = halves(jnp.concatenate([left, times_i(left)], axis=1))
    outs = (keep, send)
    for lp in range(2):
        rr = r[lp] - r[2 + lp]
        rcat = jnp.concatenate([rr[:, 0].reshape(NVEC, 2 * NVEC), rr[:, 1].reshape(NVEC, 2 * NVEC)], axis=0)
        rhi, rlo = halves(rcat)
        t = dot(lhi, rhi) + dot(llo, rhi) + dot(lhi, rlo)
        it = times_i(t)
        left = jnp.concatenate(
            [jnp.concatenate([t[:, l * NVEC:(l + 1) * NVEC], it[:, l * NVEC:(l + 1) * NVEC]], axis=1) for l in range(2)],
            axis=0,
        )
        fhi, flo = halves(left)
        nt = (((1,), (1,)), ((), ()))
        w = lax.dot_general(fhi, e_both, nt, preferred_element_type=F32)
        w = w[:, :NVEC] + w[:, NVEC:] + lax.dot_general(flo, ehi, nt, preferred_element_type=F32)
        for l in range(2):
            for n in range(2):
                outs[n][lp, l] = w[64 * l + 32 * n:64 * l + 32 * n + 32]


def dress(tp, place, e, r):
    smem = pl.BlockSpec(memory_space=pltpu.SMEM)
    vmem = pl.BlockSpec(memory_space=pltpu.VMEM)
    out = jax.ShapeDtypeStruct((2, 2, 2 * BLK, NVEC), F32)
    return pl.pallas_call(
        dress_kernel,
        out_shape=(out, out),
        in_specs=[smem, smem, vmem, vmem],
        out_specs=(vmem, vmem),
        scratch_shapes=[pltpu.VMEM((4 * BLK, NVEC), F32)],
        name="dress",
        interpret=INTERPRET,
    )(tp, place, e, r)


def shards(eigvecs, perambulator, time_pairs, momenta):
    z, y, c = lax.axis_index("z"), lax.axis_index("y"), lax.axis_index("c")
    slab = (z * 8 + y * 2 + c).reshape(1)
    place = jnp.stack([y, c])
    partial = elementals(momenta, slab, eigvecs.reshape(2 * ROWS, NVEC))
    parts = lax.all_to_all(partial.reshape(32, 2, BLK, NVEC), ("z", "y", "c"), 0, 0, tiled=True)
    fold = perambulator[..., :256] + perambulator[..., 256:]
    fold = jnp.transpose(fold, (1, 2, 0, 3))
    fold = jnp.broadcast_to(fold[None], (16, 2, 2, BLK, 256)).reshape(32, 2, BLK, 256)
    cols = lax.all_to_all(fold, ("z", "y", "c"), 0, 0, tiled=True).reshape(4, 8, 2, BLK, 256)
    rows = parts.sum(axis=0) * (1.0 / math.sqrt(2.0 * NCOL * NSITE))
    rows = jnp.broadcast_to(rows[None], (32, 2, BLK, NVEC))
    elem = lax.all_to_all(rows, ("x", "y", "c"), 0, 0, tiled=True).reshape(4, 8, 2, BLK, NVEC)
    keep, send = dress(time_pairs, place, elem, cols)
    other = lax.ppermute(send, "c", [(0, 1), (1, 0)])
    first = jnp.where(c == 0, keep, other)
    second = jnp.where(c == 0, other, keep)
    pair = jnp.stack([first, second], axis=1)
    pair = jnp.broadcast_to(pair[None], (2, *pair.shape)).reshape(4, 2, 2, 2 * BLK, NVEC)
    done = lax.all_to_all(pair, "z", 0, 0, tiled=True)
    done = done * jnp.where(z >= 2, -1.0, 1.0)
    done = done.reshape(NMOM, 2, 2, BLK, 2, NVEC).transpose(3, 1, 0, 4, 2, 5).reshape(BLK, 2, NMOM, 2, 256)
    return jnp.concatenate([done, done], axis=-1)


def solution(mesh):
    fine = Mesh(mesh.devices.reshape(4, 4, 4, 2), ("x", "z", "y", "c"))
    slab = ("z", "y", "c")
    return jax.shard_map(
        shards,
        mesh=fine,
        in_specs=(P("x", None, slab, None, None), P(slab, "x", None, None), P("x", None), P()),
        out_specs=P(slab, "x", None, None, None),
        check_vma=False,
    )
```

```python
import math

import jax
import jax.numpy as jnp
from jax import lax
from jax.experimental import pallas as pl
from jax.experimental.pallas import tpu as pltpu
from jax.sharding import Mesh
from jax.sharding import PartitionSpec as P

LS = 48
NMOM = 4
NVEC = 128
NCOL = 3
SITES = 432
ROWS = NCOL * SITES
NSITE = 13824
BLK = 16
F32 = jnp.float32
BF16 = jnp.bfloat16
INTERPRET = False


def halves(x):
    hi = x.astype(BF16)
    return hi, (x - hi.astype(F32)).astype(BF16)


def dot(a, b):
    return jnp.dot(a, b, preferred_element_type=F32)


def over48(x):
    return lax.shift_right_logical(x * 43691, 21)


def phase_rows(mom, slab):
    lane = lax.broadcasted_iota(jnp.int32, (8, ROWS), 1)
    row = lax.broadcasted_iota(jnp.int32, (8, ROWS), 0)
    site = lane - jnp.where(lane >= 2 * SITES, 2 * SITES, jnp.where(lane >= SITES, SITES, 0)) + slab * SITES
    line = over48(site)
    plane = over48(line)
    coords = (site - LS * line, line - LS * plane, plane)
    mrow = row & 3
    turns = jnp.where(row >= 4, 7 * LS - 12, 6 * LS)
    for d in range(3):
        p = jnp.where(mrow == 0, mom[0, d], jnp.where(mrow == 1, mom[1, d], jnp.where(mrow == 2, mom[2, d], mom[3, d])))
        turns = turns + p * coords[d]
    turns = turns - LS * over48(turns)
    return jnp.cos(turns.astype(F32) * (2.0 * math.pi / LS))


def elemental_kernel(mom, slab, x, o, at, bt, whi, wlo, uhi, ulo):
    tab = phase_rows(mom, slab[0])
    a = x[pl.ds(0, ROWS, stride=2), :]
    b = x[pl.ds(1, ROWS, stride=2), :]
    for n, v in enumerate((a, b)):
        hi, lo = halves(v)
        whi[:, n * NVEC:(n + 1) * NVEC] = hi
        wlo[:, n * NVEC:(n + 1) * NVEC] = lo
    at[...] = a.T
    bt[...] = b.T
    for m in range(NMOM):
        for k0 in range(0, ROWS, 128):
            ks = slice(k0, min(k0 + 128, ROWS))
            cos, sin = tab[m:m + 1, ks], tab[4 + m:5 + m, ks]
            ak, bk = at[:, ks], bt[:, ks]
            for n, u in enumerate((cos * ak + sin * bk, cos * bk - sin * ak)):
                hi, lo = halves(u)
                uhi[m, n * NVEC:(n + 1) * NVEC, ks] = hi
                ulo[m, n * NVEC:(n + 1) * NVEC, ks] = lo
        prod = dot(uhi[m], whi[...]) + dot(ulo[m], whi[...]) + dot(uhi[m], wlo[...])
        re = prod[:NVEC, :NVEC] + prod[NVEC:, NVEC:]
        im = prod[:NVEC, NVEC:] - prod[NVEC:, :NVEC]
        o[m, :, 0] = re.reshape(8, BLK, NVEC)
        o[m, :, 1] = im.reshape(8, BLK, NVEC)


def elementals(mom, slab, x):
    return pl.pallas_call(
        elemental_kernel,
        out_shape=jax.ShapeDtypeStruct((NMOM, 8, 2, BLK, NVEC), F32),
        in_specs=[
            pl.BlockSpec(memory_space=pltpu.SMEM),
            pl.BlockSpec(memory_space=pltpu.SMEM),
            pl.BlockSpec(memory_space=pltpu.VMEM),
        ],
        out_specs=pl.BlockSpec(memory_space=pltpu.VMEM),
        scratch_shapes=[
            pltpu.VMEM((NVEC, ROWS), F32),
            pltpu.VMEM((NVEC, ROWS), F32),
            pltpu.VMEM((ROWS, 2 * NVEC), BF16),
            pltpu.VMEM((ROWS, 2 * NVEC), BF16),
            pltpu.VMEM((NMOM, 2 * NVEC, ROWS), BF16),
            pltpu.VMEM((NMOM, 2 * NVEC, ROWS), BF16),
        ],
        cost_estimate=pl.CostEstimate(flops=10_000_000_000, transcendentals=0, bytes_accessed=20_000_000),
        name="elementals",
        interpret=INTERPRET,
    )(mom, slab, x)


def times_i(x):
    rows = x.shape[0]
    y = x.reshape(rows // 8, 8, x.shape[1])
    even = lax.broadcasted_iota(jnp.int32, y.shape, 1) % 2 == 0
    y = jnp.where(even, -pltpu.roll(y, 7, 1), pltpu.roll(y, 1, 1))
    return y.reshape(x.shape)


def dress_kernel(tp, place, e, *refs):
    own, far, o, lrows, cols = refs[:4], refs[4:8], refs[8], refs[9], refs[10]
    z, y, c = place[0], place[1], place[2]
    t1, t2 = tp[c, 0], tp[c, 1]
    sink = e[t2]
    cat = jnp.concatenate([sink[:, 0].reshape(NVEC, NVEC), sink[:, 1].reshape(NVEC, NVEC)], axis=1)
    ehi, elo = halves(cat)
    e_both = jnp.concatenate([ehi, elo], axis=0)
    for n in range(2):
        src = e[t1, 2 * y + n]
        lrows[pl.ds(2 * BLK * n, BLK, stride=2), :] = src[0]
        lrows[pl.ds(2 * BLK * n + 1, BLK, stride=2), :] = -src[1]
    left = lrows[...]
    lhi, llo = halves(jnp.concatenate([left, times_i(left)], axis=1))
    for n, group in enumerate((own, far)):
        for j in range(4):
            for h in range(2):
                cols[n, 2 * (y ^ j) + (c ^ h)] = group[j][h]
    low = z % 2
    for n in range(2):
        lp = low ^ n
        rr = cols[n]
        rcat = jnp.concatenate([rr[:, 0].reshape(NVEC, 2 * NVEC), rr[:, 1].reshape(NVEC, 2 * NVEC)], axis=0)
        rhi, rlo = halves(rcat)
        t = dot(lhi, rhi) + dot(llo, rhi) + dot(lhi, rlo)
        it = times_i(t)
        left = jnp.concatenate(
            [jnp.concatenate([t[:, l * NVEC:(l + 1) * NVEC], it[:, l * NVEC:(l + 1) * NVEC]], axis=1) for l in range(2)],
            axis=0,
        )
        fhi, flo = halves(left)
        nt = (((1,), (1,)), ((), ()))
        w = lax.dot_general(fhi, e_both, nt, preferred_element_type=F32)
        w = w[:, :NVEC] + w[:, NVEC:] + lax.dot_general(flo, ehi, nt, preferred_element_type=F32)
        for l in range(2):
            for h in range(2):
                part = w[64 * l + 32 * h:64 * l + 32 * h + 32]
                o[lp, h, l] = part
                o[2 + lp, h, l] = -part


def dress(tp, place, e, own, far):
    smem = pl.BlockSpec(memory_space=pltpu.SMEM)
    vmem = pl.BlockSpec(memory_space=pltpu.VMEM)
    return pl.pallas_call(
        dress_kernel,
        out_shape=jax.ShapeDtypeStruct((4, 2, 2, 2 * BLK, NVEC), F32),
        in_specs=[smem, smem] + [vmem] * 9,
        out_specs=vmem,
        scratch_shapes=[pltpu.VMEM((4 * BLK, NVEC), F32), pltpu.VMEM((2, 8, 2, BLK, 2 * NVEC), F32)],
        name="dress",
        interpret=INTERPRET,
    )(tp, place, e, *own, *far)


def swapped(x, axis, bits):
    size = 4 if axis in ("z", "y") else 2 if axis == "c" else 8
    return lax.ppermute(x, axis, [(i, i ^ bits) for i in range(size)])


def shards(eigvecs, perambulator, time_pairs, momenta):
    z, y, c = lax.axis_index("z"), lax.axis_index("y"), lax.axis_index("c")
    slab = (z * 8 + y * 2 + c).reshape(1)
    place = jnp.stack([z, y, c])
    partial = elementals(momenta, slab, eigvecs.reshape(2 * ROWS, NVEC))
    partial, perambulator = lax.optimization_barrier((partial, perambulator))
    parts = lax.all_to_all(partial.reshape(32, 2, BLK, NVEC), ("z", "y", "c"), 0, 0, tiled=True)
    fold = perambulator[..., :256] + perambulator[..., 256:]
    fold = jnp.transpose(fold, (1, 2, 0, 3))
    mine = lax.dynamic_index_in_dim(fold, c, 0, keepdims=False)
    theirs = lax.dynamic_index_in_dim(fold, 1 - c, 0, keepdims=False)
    sign = jnp.where(z < 2, 1.0, -1.0)
    cols = jnp.stack([
        sign * (mine - swapped(mine, "z", 2)),
        sign * (swapped(theirs, "c", 1) - swapped(theirs, ("z", "c"), 5)),
    ])
    own = [cols] + [swapped(cols, "y", j) for j in (1, 2, 3)]
    parts, own = lax.optimization_barrier((parts, own))
    rows = parts.sum(axis=0) * (1.0 / math.sqrt(2.0 * NCOL * NSITE))
    rows = jnp.broadcast_to(rows[None], (32, 2, BLK, NVEC))
    elem = lax.all_to_all(rows, ("x", "y", "c"), 0, 0, tiled=True).reshape(4, 8, 2, BLK, NVEC)
    far = [swapped(v, "z", 1) for v in own]
    pieces = dress(time_pairs, place, elem, own, far)
    done = lax.all_to_all(pieces.reshape(8, 2, 2 * BLK, NVEC), ("z", "c"), 0, 0, tiled=True)
    done = done.reshape(NMOM, 2, 2, BLK, 2, NVEC).transpose(3, 1, 0, 4, 2, 5).reshape(BLK, 2, NMOM, 2, 256)
    return jnp.concatenate([done, done], axis=-1)


def solution(mesh):
    fine = Mesh(mesh.devices.reshape(4, 4, 4, 2), ("x", "z", "y", "c"))
    slab = ("z", "y", "c")
    return jax.shard_map(
        shards,
        mesh=fine,
        in_specs=(P("x", None, slab, None, None), P(slab, "x", None, None), P("x", None), P()),
        out_specs=P(slab, "x", None, None, None),
        check_vma=False,
    )
```

```python
import math

import jax
import jax.numpy as jnp
from jax import lax
from jax.experimental import pallas as pl
from jax.experimental.pallas import tpu as pltpu
from jax.sharding import Mesh
from jax.sharding import PartitionSpec as P

LS = 48
NMOM = 4
NVEC = 128
NCOL = 3
SITES = 432
ROWS = NCOL * SITES
FULL = 1280
NSITE = 13824
BLK = 16
F32 = jnp.float32
BF16 = jnp.bfloat16


def halves(x):
    hi = x.astype(BF16)
    return hi, (x - hi.astype(F32)).astype(BF16)


def dot(a, b):
    return jnp.dot(a, b, preferred_element_type=F32)


def over48(x):
    return lax.shift_right_logical(x * 43691, 21)


def phase_rows(mom, slab, lanes, first, period):
    lane = lax.broadcasted_iota(jnp.int32, (8, lanes), 1) % period + first
    row = lax.broadcasted_iota(jnp.int32, (8, lanes), 0)
    site = lane - jnp.where(lane >= 2 * SITES, 2 * SITES, jnp.where(lane >= SITES, SITES, 0)) + slab * SITES
    line = over48(site)
    plane = over48(line)
    coords = (site - LS * line, line - LS * plane, plane)
    mrow = row & 3
    turns = jnp.where(row >= 4, 7 * LS - 12, 6 * LS)
    for d in range(3):
        p = jnp.where(mrow == 0, mom[0, d], jnp.where(mrow == 1, mom[1, d], jnp.where(mrow == 2, mom[2, d], mom[3, d])))
        turns = turns + p * coords[d]
    turns = turns - LS * over48(turns)
    return jnp.cos(turns.astype(F32) * (2.0 * math.pi / LS))


def turned(tab, m, at, bt):
    cos, sin = tab[m:m + 1], tab[4 + m:5 + m]
    return jnp.concatenate([cos * at + sin * bt, cos * bt - sin * at], axis=0)


def elemental_kernel(mom, slab, x, o):
    tab = phase_rows(mom, slab[0], FULL, 0, FULL)
    tail = phase_rows(mom, slab[0], 3 * BLK, FULL, BLK)
    a = x[pl.ds(2 * FULL, BLK, stride=2), :]
    b = x[pl.ds(2 * FULL + 1, BLK, stride=2), :]
    whi, wlo = halves(jnp.concatenate([a, b], axis=1))
    w = jnp.concatenate([whi, whi, wlo], axis=0)
    at = jnp.concatenate([a, a, a], axis=0).T
    bt = jnp.concatenate([b, b, b], axis=0).T
    lane = lax.broadcasted_iota(jnp.int32, (2 * NVEC, 3 * BLK), 1)
    middle = (lane >= BLK) & (lane < 2 * BLK)
    total = []
    for m in range(NMOM):
        u = turned(tail, m, at, bt)
        hi = u.astype(BF16).astype(F32)
        total.append(dot(jnp.where(middle, u - hi, hi).astype(BF16), w))
    for k0 in range(0, FULL, 256):
        a = x[pl.ds(2 * k0, 256, stride=2), :]
        b = x[pl.ds(2 * k0 + 1, 256, stride=2), :]
        whi, wlo = halves(jnp.concatenate([a, b], axis=1))
        at, bt = a.T, b.T
        for m in range(NMOM):
            hi, lo = halves(turned(tab[:, k0:k0 + 256], m, at, bt))
            total[m] = total[m] + (dot(hi, whi) + dot(lo, whi) + dot(hi, wlo))
    for m in range(NMOM):
        re = total[m][:NVEC, :NVEC] + total[m][NVEC:, NVEC:]
        im = total[m][:NVEC, NVEC:] - total[m][NVEC:, :NVEC]
        o[m, :, 0] = re.reshape(8, BLK, NVEC)
        o[m, :, 1] = im.reshape(8, BLK, NVEC)


def elementals(mom, slab, x):
    return pl.pallas_call(
        elemental_kernel,
        out_shape=jax.ShapeDtypeStruct((NMOM, 8, 2, BLK, NVEC), F32),
        in_specs=[
            pl.BlockSpec(memory_space=pltpu.SMEM),
            pl.BlockSpec(memory_space=pltpu.SMEM),
            pl.BlockSpec(memory_space=pltpu.VMEM),
        ],
        out_specs=pl.BlockSpec(memory_space=pltpu.VMEM),
        cost_estimate=pl.CostEstimate(flops=10_000_000_000, transcendentals=0, bytes_accessed=20_000_000),
        name="elementals",
    )(mom, slab, x)


def times_i(x):
    rows = x.shape[0]
    y = x.reshape(rows // 8, 8, x.shape[1])
    even = lax.broadcasted_iota(jnp.int32, y.shape, 1) % 2 == 0
    y = jnp.where(even, -pltpu.roll(y, 7, 1), pltpu.roll(y, 1, 1))
    return y.reshape(x.shape)


def dress_kernel(tp, place, e, *refs):
    own, far, outs, lrows, cols = refs[:4], refs[4:8], refs[8:10], refs[10], refs[11]
    z, y, c = place[0], place[1], place[2]
    t1, t2 = tp[c, 0], tp[c, 1]
    sink = e[t2]
    cat = jnp.concatenate([sink[:, 0].reshape(NVEC, NVEC), sink[:, 1].reshape(NVEC, NVEC)], axis=1)
    ehi, elo = halves(cat)
    e_both = jnp.concatenate([ehi, elo], axis=0)
    for n in range(2):
        src = e[t1, 2 * y + (c ^ n)]
        lrows[pl.ds(2 * BLK * n, BLK, stride=2), :] = src[0]
        lrows[pl.ds(2 * BLK * n + 1, BLK, stride=2), :] = -src[1]
    left = lrows[...]
    lhi, llo = halves(jnp.concatenate([left, times_i(left)], axis=1))
    for n, group in enumerate((own, far)):
        for j in range(4):
            for h in range(2):
                cols[n, 2 * (y ^ j) + (c ^ h)] = group[j][h]
    for n in range(2):
        rr = cols[n]
        rcat = jnp.concatenate([rr[:, 0].reshape(NVEC, 2 * NVEC), rr[:, 1].reshape(NVEC, 2 * NVEC)], axis=0)
        rhi, rlo = halves(rcat)
        t = dot(lhi, rhi) + dot(llo, rhi) + dot(lhi, rlo)
        it = times_i(t)
        left = jnp.concatenate(
            [jnp.concatenate([t[:, l * NVEC:(l + 1) * NVEC], it[:, l * NVEC:(l + 1) * NVEC]], axis=1) for l in range(2)],
            axis=0,
        )
        fhi, flo = halves(left)
        nt = (((1,), (1,)), ((), ()))
        w = lax.dot_general(fhi, e_both, nt, preferred_element_type=F32)
        w = w[:, :NVEC] + w[:, NVEC:] + lax.dot_general(flo, ehi, nt, preferred_element_type=F32)
        for l in range(2):
            for h in range(2):
                outs[n][h, l] = w[64 * l + 32 * h:64 * l + 32 * h + 32]


def dress(tp, place, e, own, far):
    smem = pl.BlockSpec(memory_space=pltpu.SMEM)
    vmem = pl.BlockSpec(memory_space=pltpu.VMEM)
    e, *blocks = [pltpu.with_memory_space_constraint(v, pltpu.VMEM) for v in (e, *own, *far)]
    return pl.pallas_call(
        dress_kernel,
        out_shape=[pltpu.VMEM((2, 2, 2 * BLK, NVEC), F32)] * 2,
        in_specs=[smem, smem] + [vmem] * 9,
        out_specs=[vmem] * 2,
        scratch_shapes=[pltpu.VMEM((4 * BLK, NVEC), F32), pltpu.VMEM((2, 8, 2, BLK, 2 * NVEC), F32)],
        name="dress",
    )(tp, place, e, *blocks)


def spread_kernel(parts, o):
    total = parts[0]
    for n in range(1, 32):
        total = total + parts[n]
    total = total * (1.0 / math.sqrt(2.0 * NCOL * NSITE))
    for n in range(32):
        o[n] = total


def spread(parts):
    vmem = pl.BlockSpec(memory_space=pltpu.VMEM)
    return pl.pallas_call(
        spread_kernel,
        out_shape=pltpu.VMEM((32, 2, BLK, NVEC), F32),
        in_specs=[vmem],
        out_specs=vmem,
        name="spread",
    )(pltpu.with_memory_space_constraint(parts, pltpu.VMEM))


def swapped(x, axis, bits):
    size = 4 if axis in ("z", "y") else 2 if axis == "c" else 8
    return lax.ppermute(x, axis, [(i, i ^ bits) for i in range(size)])


def assemble_kernel(place, *refs):
    z, c = place[0], place[2]
    out = refs[8]
    sign = jnp.where(z >= 2, -1.0, 1.0)
    for n in range(2):
        for j in range(4):
            for l in range(2):
                part = (refs[4 * n + j][n, l] * sign).reshape(BLK, 2, NVEC)
                for v in range(2):
                    out[:, c ^ n, z ^ j, :, 256 * v + NVEC * l:256 * v + NVEC * (l + 1)] = part


def assemble(place, keep, other):
    vmem = pl.BlockSpec(memory_space=pltpu.VMEM)
    return pl.pallas_call(
        assemble_kernel,
        out_shape=jax.ShapeDtypeStruct((BLK, 2, NMOM, 2, 512), F32),
        in_specs=[pl.BlockSpec(memory_space=pltpu.SMEM)] + [vmem] * 8,
        out_specs=vmem,
        name="assemble",
    )(place, *[pltpu.with_memory_space_constraint(v, pltpu.VMEM) for v in (*keep, *other)])


def shards(eigvecs, perambulator, time_pairs, momenta):
    z, y, c = lax.axis_index("z"), lax.axis_index("y"), lax.axis_index("c")
    slab = (z * 8 + y * 2 + c).reshape(1)
    place = jnp.stack([z, y, c])
    partial = elementals(momenta, slab, eigvecs.reshape(2 * ROWS, NVEC))
    partial, perambulator = lax.optimization_barrier((partial, perambulator))
    parts = lax.all_to_all(partial.reshape(32, 2, BLK, NVEC), ("z", "y", "c"), 0, 0, tiled=True)
    fold = perambulator[..., :256] + perambulator[..., 256:]
    fold = jnp.transpose(fold, (1, 2, 0, 3))
    mine = lax.dynamic_index_in_dim(fold, c, 0, keepdims=False)
    theirs = lax.dynamic_index_in_dim(fold, 1 - c, 0, keepdims=False)
    sign = jnp.where(z < 2, 1.0, -1.0)
    cols = jnp.stack([
        sign * (mine - swapped(mine, "z", 2)),
        sign * (swapped(theirs, "c", 1) - swapped(theirs, ("z", "c"), 5)),
    ])
    own = [cols] + [swapped(cols, "y", j) for j in (1, 2, 3)]
    parts, own = lax.optimization_barrier((parts, own))
    elem = lax.all_to_all(spread(parts), ("x", "y", "c"), 0, 0, tiled=True).reshape(4, 8, 2, BLK, NVEC)
    far = [swapped(v, "z", 1) for v in own]
    near, far = dress(time_pairs, place, elem, own, far)
    keep = [near, swapped(far, "z", 1), swapped(near, "z", 2), swapped(far, "z", 3)]
    return assemble(place, keep, [swapped(v, "c", 1) for v in keep])


def solution(mesh):
    fine = Mesh(mesh.devices.reshape(4, 4, 4, 2), ("x", "z", "y", "c"))
    slab = ("z", "y", "c")
    return jax.shard_map(
        shards,
        mesh=fine,
        in_specs=(P("x", None, slab, None, None), P(slab, "x", None, None), P("x", None), P()),
        out_specs=P(slab, "x", None, None, None),
        check_vma=False,
    )
```

```python
import math

import jax
import jax.numpy as jnp
from jax import lax
from jax.experimental import pallas as pl
from jax.experimental.pallas import tpu as pltpu
from jax.sharding import Mesh
from jax.sharding import PartitionSpec as P

LS = 48
NMOM = 4
NVEC = 128
NCOL = 3
SITES = 432
ROWS = NCOL * SITES
FULL = 1280
NSITE = 13824
BLK = 16
F32 = jnp.float32
BF16 = jnp.bfloat16


def halves(x):
    hi = x.astype(BF16)
    return hi, (x - hi.astype(F32)).astype(BF16)


def dot(a, b):
    return jnp.dot(a, b, preferred_element_type=F32)


def over48(x):
    return lax.shift_right_logical(x * 43691, 21)


def phase_rows(mom, slab, lanes, first, period):
    lane = lax.broadcasted_iota(jnp.int32, (8, lanes), 1) % period + first
    row = lax.broadcasted_iota(jnp.int32, (8, lanes), 0)
    site = lane - jnp.where(lane >= 2 * SITES, 2 * SITES, jnp.where(lane >= SITES, SITES, 0)) + slab * SITES
    line = over48(site)
    plane = over48(line)
    coords = (site - LS * line, line - LS * plane, plane)
    mrow = row & 3
    turns = jnp.where(row >= 4, 7 * LS - 12, 6 * LS)
    for d in range(3):
        p = jnp.where(mrow == 0, mom[0, d], jnp.where(mrow == 1, mom[1, d], jnp.where(mrow == 2, mom[2, d], mom[3, d])))
        turns = turns + p * coords[d]
    turns = turns - LS * over48(turns)
    return jnp.cos(turns.astype(F32) * (2.0 * math.pi / LS))


def turned(tab, m, at, bt):
    cos, sin = tab[m:m + 1], tab[4 + m:5 + m]
    return jnp.concatenate([cos * at + sin * bt, cos * bt - sin * at], axis=0)


def elemental_kernel(mom, slab, core, x, keep, send):
    tab = phase_rows(mom, slab[0], FULL, 0, FULL)
    tail = phase_rows(mom, slab[0], 3 * BLK, FULL, BLK)
    a = x[pl.ds(2 * FULL, BLK, stride=2), :]
    b = x[pl.ds(2 * FULL + 1, BLK, stride=2), :]
    whi, wlo = halves(jnp.concatenate([a, b], axis=1))
    w = jnp.concatenate([whi, whi, wlo], axis=0)
    at = jnp.concatenate([a, a, a], axis=0).T
    bt = jnp.concatenate([b, b, b], axis=0).T
    lane = lax.broadcasted_iota(jnp.int32, (2 * NVEC, 3 * BLK), 1)
    middle = (lane >= BLK) & (lane < 2 * BLK)
    total = []
    for m in range(NMOM):
        u = turned(tail, m, at, bt)
        hi = u.astype(BF16).astype(F32)
        total.append(dot(jnp.where(middle, u - hi, hi).astype(BF16), w))
    for k0 in range(0, FULL, 256):
        a = x[pl.ds(2 * k0, 256, stride=2), :]
        b = x[pl.ds(2 * k0 + 1, 256, stride=2), :]
        whi, wlo = halves(jnp.concatenate([a, b], axis=1))
        at, bt = a.T, b.T
        for m in range(NMOM):
            hi, lo = halves(turned(tab[:, k0:k0 + 256], m, at, bt))
            total[m] = total[m] + (dot(hi, whi) + dot(lo, whi) + dot(hi, wlo))
    for m in range(NMOM):
        re = total[m][:NVEC, :NVEC] + total[m][NVEC:, NVEC:]
        im = total[m][:NVEC, NVEC:] - total[m][NVEC:, :NVEC]
        for n, part in enumerate((re, im)):
            part = part.reshape(4, 2, BLK, NVEC)
            first, second = part[:, 0], part[:, 1]
            odd = core[0] == 1
            keep[m, :, n] = jnp.where(odd, second, first)
            send[m, :, n] = jnp.where(odd, first, second)


def elementals(mom, slab, core, x):
    return pl.pallas_call(
        elemental_kernel,
        out_shape=[pltpu.VMEM((NMOM, 4, 2, BLK, NVEC), F32)] * 2,
        in_specs=[
            pl.BlockSpec(memory_space=pltpu.SMEM),
            pl.BlockSpec(memory_space=pltpu.SMEM),
            pl.BlockSpec(memory_space=pltpu.SMEM),
            pl.BlockSpec(memory_space=pltpu.VMEM),
        ],
        out_specs=[pl.BlockSpec(memory_space=pltpu.VMEM)] * 2,
        cost_estimate=pl.CostEstimate(flops=10_000_000_000, transcendentals=0, bytes_accessed=20_000_000),
        name="elementals",
    )(mom, slab, core, x)


def times_i(x):
    rows = x.shape[0]
    y = x.reshape(rows // 8, 8, x.shape[1])
    even = lax.broadcasted_iota(jnp.int32, y.shape, 1) % 2 == 0
    y = jnp.where(even, -pltpu.roll(y, 7, 1), pltpu.roll(y, 1, 1))
    return y.reshape(x.shape)


def dress_kernel(tp, yat, cat, *refs):
    elem, refs = refs[:2], refs[2:]
    own, far, outs, lrows, cols = refs[:4], refs[4:8], refs[8:10], refs[10], refs[11]
    rows = refs[12]
    y, c = yat[0], cat[0]
    t1, t2 = tp[c, 0], tp[c, 1]
    for h in range(2):
        for yy in range(4):
            rows[2 * yy + (c ^ h)] = elem[h][t2, yy]
    sink = rows[...]
    both = jnp.concatenate([sink[:, 0].reshape(NVEC, NVEC), sink[:, 1].reshape(NVEC, NVEC)], axis=1)
    ehi, elo = halves(both)
    e_both = jnp.concatenate([ehi, elo], axis=0)
    for n in range(2):
        src = elem[n][t1, y]
        lrows[pl.ds(2 * BLK * n, BLK, stride=2), :] = src[0]
        lrows[pl.ds(2 * BLK * n + 1, BLK, stride=2), :] = -src[1]
    left = lrows[...]
    lhi, llo = halves(jnp.concatenate([left, times_i(left)], axis=1))
    for n, group in enumerate((own, far)):
        for j in range(4):
            for h in range(2):
                cols[n, 2 * (y ^ j) + (c ^ h)] = group[j][h]
    for n in range(2):
        rr = cols[n]
        rcat = jnp.concatenate([rr[:, 0].reshape(NVEC, 2 * NVEC), rr[:, 1].reshape(NVEC, 2 * NVEC)], axis=0)
        rhi, rlo = halves(rcat)
        t = dot(lhi, rhi) + dot(llo, rhi) + dot(lhi, rlo)
        it = times_i(t)
        left = jnp.concatenate(
            [jnp.concatenate([t[:, l * NVEC:(l + 1) * NVEC], it[:, l * NVEC:(l + 1) * NVEC]], axis=1) for l in range(2)],
            axis=0,
        )
        fhi, flo = halves(left)
        nt = (((1,), (1,)), ((), ()))
        w = lax.dot_general(fhi, e_both, nt, preferred_element_type=F32)
        w = w[:, :NVEC] + w[:, NVEC:] + lax.dot_general(flo, ehi, nt, preferred_element_type=F32)
        for l in range(2):
            for h in range(2):
                outs[n][h, l] = w[64 * l + 32 * h:64 * l + 32 * h + 32]


def dress(tp, at, elem, own, far):
    smem = pl.BlockSpec(memory_space=pltpu.SMEM)
    vmem = pl.BlockSpec(memory_space=pltpu.VMEM)
    blocks = [pltpu.with_memory_space_constraint(v, pltpu.VMEM) for v in (*elem, *own, *far)]
    return pl.pallas_call(
        dress_kernel,
        out_shape=[pltpu.VMEM((2, 2, 2 * BLK, NVEC), F32)] * 2,
        in_specs=[smem, smem, smem] + [vmem] * 10,
        out_specs=[vmem] * 2,
        scratch_shapes=[pltpu.VMEM((4 * BLK, NVEC), F32), pltpu.VMEM((2, 8, 2, BLK, 2 * NVEC), F32), pltpu.VMEM((8, 2, BLK, NVEC), F32)],
        name="dress",
    )(tp, at[1], at[2], *blocks)


def spread_kernel(parts, o):
    total = parts[0]
    for n in range(1, 16):
        total = total + parts[n]
    total = total * (1.0 / math.sqrt(2.0 * NCOL * NSITE))
    for n in range(16):
        o[n] = total


def spread(parts):
    vmem = pl.BlockSpec(memory_space=pltpu.VMEM)
    return pl.pallas_call(
        spread_kernel,
        out_shape=pltpu.VMEM((16, 2, BLK, NVEC), F32),
        in_specs=[vmem],
        out_specs=vmem,
        name="spread",
    )(pltpu.with_memory_space_constraint(parts, pltpu.VMEM))


def swapped(x, axis, bits):
    size = 4 if axis in ("z", "y") else 2 if axis == "c" else 8
    return lax.ppermute(x, axis, [(i, i ^ bits) for i in range(size)])


def assemble_kernel(zat, cat, *refs):
    z, c = zat[0], cat[0]
    out = refs[8]
    sign = jnp.where(z >= 2, -1.0, 1.0)
    for n in range(2):
        for j in range(4):
            for l in range(2):
                part = (refs[4 * n + j][n, l] * sign).reshape(BLK, 2, NVEC)
                for v in range(2):
                    out[:, c ^ n, z ^ j, :, 256 * v + NVEC * l:256 * v + NVEC * (l + 1)] = part


def assemble(at, keep, other):
    vmem = pl.BlockSpec(memory_space=pltpu.VMEM)
    return pl.pallas_call(
        assemble_kernel,
        out_shape=jax.ShapeDtypeStruct((BLK, 2, NMOM, 2, 512), F32),
        in_specs=[pl.BlockSpec(memory_space=pltpu.SMEM)] * 2 + [vmem] * 8,
        out_specs=vmem,
        name="assemble",
    )(at[0], at[2], *[pltpu.with_memory_space_constraint(v, pltpu.VMEM) for v in (*keep, *other)])


def shards(eigvecs, perambulator, time_pairs, momenta):
    z, y, c = lax.axis_index("z"), lax.axis_index("y"), lax.axis_index("c")
    slab = (z * 8 + y * 2 + c).reshape(1)
    at = (z.reshape(1), y.reshape(1), c.reshape(1))
    partial, send = elementals(momenta, slab, at[2], eigvecs.reshape(2 * ROWS, NVEC))
    partial = partial + swapped(send, "c", 1)
    partial, perambulator = lax.optimization_barrier((partial, perambulator))
    parts = lax.all_to_all(partial.reshape(16, 2, BLK, NVEC), ("z", "y"), 0, 0, tiled=True)
    fold = perambulator[..., :256] + perambulator[..., 256:]
    fold = jnp.transpose(fold, (1, 2, 0, 3))
    mine = lax.dynamic_index_in_dim(fold, c, 0, keepdims=False)
    theirs = lax.dynamic_index_in_dim(fold, 1 - c, 0, keepdims=False)
    sign = jnp.where(z < 2, 1.0, -1.0)
    cols = jnp.stack([
        sign * (mine - swapped(mine, "z", 2)),
        sign * (swapped(theirs, "c", 1) - swapped(theirs, ("z", "c"), 5)),
    ])
    own = [cols] + [swapped(cols, "y", j) for j in (1, 2, 3)]
    parts, own = lax.optimization_barrier((parts, own))
    elem = lax.all_to_all(spread(parts), ("x", "y"), 0, 0, tiled=True).reshape(4, 4, 2, BLK, NVEC)
    far = [swapped(v, "z", 1) for v in own]
    elem, far = lax.optimization_barrier((elem, far))
    elem = (elem, swapped(elem, "c", 1))
    near, far = dress(time_pairs, at, elem, own, far)
    keep = [near, swapped(far, "z", 1), swapped(near, "z", 2), swapped(far, "z", 3)]
    return assemble(at, keep, [swapped(v, "c", 1) for v in keep])


def solution(mesh):
    fine = Mesh(mesh.devices.reshape(4, 4, 4, 2), ("x", "z", "y", "c"))
    slab = ("z", "y", "c")
    return jax.shard_map(
        shards,
        mesh=fine,
        in_specs=(P("x", None, slab, None, None), P(slab, "x", None, None), P("x", None), P()),
        out_specs=P(slab, "x", None, None, None),
        check_vma=False,
    )
```

```python
import math

import jax
import jax.numpy as jnp
from jax import lax
from jax.experimental import pallas as pl
from jax.experimental.pallas import tpu as pltpu
from jax.sharding import Mesh
from jax.sharding import PartitionSpec as P

LS = 48
NMOM = 4
NVEC = 128
NCOL = 3
SITES = 432
ROWS = NCOL * SITES
FULL = 1280
NSITE = 13824
BLK = 16
F32 = jnp.float32
BF16 = jnp.bfloat16


def halves(x):
    hi = x.astype(BF16)
    return hi, (x - hi.astype(F32)).astype(BF16)


def dot(a, b):
    return jnp.dot(a, b, preferred_element_type=F32)


def over48(x):
    return lax.shift_right_logical(x * 43691, 21)


def phase_rows(mom, slab, lanes, first, period):
    lane = lax.broadcasted_iota(jnp.int32, (8, lanes), 1) % period + first
    row = lax.broadcasted_iota(jnp.int32, (8, lanes), 0)
    site = lane - jnp.where(lane >= 2 * SITES, 2 * SITES, jnp.where(lane >= SITES, SITES, 0)) + slab * SITES
    line = over48(site)
    plane = over48(line)
    coords = (site - LS * line, line - LS * plane, plane)
    mrow = row & 3
    turns = jnp.where(row >= 4, 7 * LS - 12, 6 * LS)
    for d in range(3):
        p = jnp.where(mrow == 0, mom[0, d], jnp.where(mrow == 1, mom[1, d], jnp.where(mrow == 2, mom[2, d], mom[3, d])))
        turns = turns + p * coords[d]
    turns = turns - LS * over48(turns)
    return jnp.cos(turns.astype(F32) * (2.0 * math.pi / LS))


def turned(tab, m, at, bt):
    cos, sin = tab[m:m + 1], tab[4 + m:5 + m]
    return jnp.concatenate([cos * at + sin * bt, cos * bt - sin * at], axis=0)


def elemental_kernel(mom, slab, core, x, keep, send):
    tab = phase_rows(mom, slab[0], FULL, 0, FULL)
    tail = phase_rows(mom, slab[0], 3 * BLK, FULL, BLK)
    a = x[pl.ds(2 * FULL, BLK, stride=2), :]
    b = x[pl.ds(2 * FULL + 1, BLK, stride=2), :]
    whi, wlo = halves(jnp.concatenate([a, b], axis=1))
    w = jnp.concatenate([whi, whi, wlo], axis=0)
    at = jnp.concatenate([a, a, a], axis=0).T
    bt = jnp.concatenate([b, b, b], axis=0).T
    lane = lax.broadcasted_iota(jnp.int32, (2 * NVEC, 3 * BLK), 1)
    middle = (lane >= BLK) & (lane < 2 * BLK)
    total = []
    for m in range(NMOM):
        u = turned(tail, m, at, bt)
        hi = u.astype(BF16).astype(F32)
        total.append(dot(jnp.where(middle, u - hi, hi).astype(BF16), w))
    for k0 in range(0, FULL, 256):
        a = x[pl.ds(2 * k0, 256, stride=2), :]
        b = x[pl.ds(2 * k0 + 1, 256, stride=2), :]
        whi, wlo = halves(jnp.concatenate([a, b], axis=1))
        at, bt = a.T, b.T
        for m in range(NMOM):
            hi, lo = halves(turned(tab[:, k0:k0 + 256], m, at, bt))
            total[m] = total[m] + (dot(hi, whi) + dot(lo, whi) + dot(hi, wlo))
    for m in range(NMOM):
        re = total[m][:NVEC, :NVEC] + total[m][NVEC:, NVEC:]
        im = total[m][:NVEC, NVEC:] - total[m][NVEC:, :NVEC]
        for n, part in enumerate((re, im)):
            part = part.reshape(4, 2, BLK, NVEC)
            first, second = part[:, 0], part[:, 1]
            odd = core[0] == 1
            keep[m, :, n] = jnp.where(odd, second, first)
            send[m, :, n] = jnp.where(odd, first, second)


def elementals(mom, slab, core, x):
    return pl.pallas_call(
        elemental_kernel,
        out_shape=[pltpu.VMEM((NMOM, 4, 2, BLK, NVEC), F32)] * 2,
        in_specs=[
            pl.BlockSpec(memory_space=pltpu.SMEM),
            pl.BlockSpec(memory_space=pltpu.SMEM),
            pl.BlockSpec(memory_space=pltpu.SMEM),
            pl.BlockSpec(memory_space=pltpu.VMEM),
        ],
        out_specs=[pl.BlockSpec(memory_space=pltpu.VMEM)] * 2,
        cost_estimate=pl.CostEstimate(flops=10_000_000_000, transcendentals=0, bytes_accessed=20_000_000),
        name="elementals",
    )(mom, slab, core, x)


def times_i(x):
    rows = x.shape[0]
    y = x.reshape(rows // 8, 8, x.shape[1])
    even = lax.broadcasted_iota(jnp.int32, y.shape, 1) % 2 == 0
    y = jnp.where(even, -pltpu.roll(y, 7, 1), pltpu.roll(y, 1, 1))
    return y.reshape(x.shape)


def dress_kernel(tp, yat, cat, mine, theirs, *refs):
    blocks, outs, lrows, cols, rows = refs[:4], refs[4:6], refs[6], refs[7], refs[8]
    elem = (mine, theirs)
    y, c = yat[0], cat[0]
    t1, t2 = tp[c, 0], tp[c, 1]
    for j in range(4):
        for h in range(2):
            cols[2 * (y ^ j) + (c ^ h)] = blocks[j][h]
    rr = cols[...]
    rcat = jnp.concatenate([rr[:, 0].reshape(NVEC, 2 * NVEC), rr[:, 1].reshape(NVEC, 2 * NVEC)], axis=0)
    rhi, rlo = halves(rcat)
    for m in range(2):
        for h in range(2):
            src = elem[h][t1, m, y]
            first = 64 * m + 32 * h
            lrows[pl.ds(first, BLK, stride=2), :] = src[0]
            lrows[pl.ds(first + 1, BLK, stride=2), :] = -src[1]
    left = lrows[...]
    lhi, llo = halves(jnp.concatenate([left, times_i(left)], axis=1))
    t = dot(lhi, rhi) + dot(llo, rhi) + dot(lhi, rlo)
    it = times_i(t)
    for m in range(2):
        for h in range(2):
            for yy in range(4):
                rows[m, 2 * yy + (c ^ h)] = elem[h][t2, m, yy]
        sink = rows[m]
        both = jnp.concatenate([sink[:, 0].reshape(NVEC, NVEC), sink[:, 1].reshape(NVEC, NVEC)], axis=1)
        ehi, elo = halves(both)
        e_both = jnp.concatenate([ehi, elo], axis=0)
        tm, im = t[64 * m:64 * m + 64], it[64 * m:64 * m + 64]
        left = jnp.concatenate(
            [jnp.concatenate([tm[:, l * NVEC:(l + 1) * NVEC], im[:, l * NVEC:(l + 1) * NVEC]], axis=1) for l in range(2)],
            axis=0,
        )
        fhi, flo = halves(left)
        nt = (((1,), (1,)), ((), ()))
        w = lax.dot_general(fhi, e_both, nt, preferred_element_type=F32)
        w = w[:, :NVEC] + w[:, NVEC:] + lax.dot_general(flo, ehi, nt, preferred_element_type=F32)
        for l in range(2):
            for h in range(2):
                outs[h][m, l] = w[64 * l + 32 * h:64 * l + 32 * h + 32]


def dress(tp, at, elem, cols):
    smem = pl.BlockSpec(memory_space=pltpu.SMEM)
    vmem = pl.BlockSpec(memory_space=pltpu.VMEM)
    return pl.pallas_call(
        dress_kernel,
        out_shape=[pltpu.VMEM((2, 2, 2 * BLK, NVEC), F32)] * 2,
        in_specs=[smem, smem, smem] + [vmem] * 6,
        out_specs=[vmem] * 2,
        scratch_shapes=[
            pltpu.VMEM((8 * BLK, NVEC), F32),
            pltpu.VMEM((8, 2, BLK, 2 * NVEC), F32),
            pltpu.VMEM((2, 8, 2, BLK, NVEC), F32),
        ],
        name="dress",
    )(tp, at[1], at[2], *[pltpu.with_memory_space_constraint(v, pltpu.VMEM) for v in (*elem, *cols)])


def spread_kernel(parts, o):
    total = parts[0]
    for n in range(1, 16):
        total = total + parts[n]
    total = total * (1.0 / math.sqrt(2.0 * NCOL * NSITE))
    for n in range(32):
        o[n] = total


def spread(parts):
    vmem = pl.BlockSpec(memory_space=pltpu.VMEM)
    return pl.pallas_call(
        spread_kernel,
        out_shape=pltpu.VMEM((32, 2, BLK, NVEC), F32),
        in_specs=[vmem],
        out_specs=vmem,
        name="spread",
    )(pltpu.with_memory_space_constraint(parts, pltpu.VMEM))


def swapped(x, axis, bits=1):
    size = 2 if axis in ("c", "zh") else 4
    return lax.ppermute(x, axis, [(i, i ^ bits) for i in range(size)])


def assemble_kernel(hat, cat, *refs):
    high, c = hat[0], cat[0]
    out = refs[4]
    sign = jnp.where(high == 1, -1.0, 1.0)
    for n in range(2):
        for j in range(2):
            for m in range(2):
                for l in range(2):
                    part = (refs[2 * n + j][m, l] * sign).reshape(BLK, 2, NVEC)
                    for v in range(2):
                        out[:, c ^ n, 2 * (high ^ j) + m, :, 256 * v + NVEC * l:256 * v + NVEC * (l + 1)] = part


def assemble(at, keep, other):
    vmem = pl.BlockSpec(memory_space=pltpu.VMEM)
    return pl.pallas_call(
        assemble_kernel,
        out_shape=jax.ShapeDtypeStruct((BLK, 2, NMOM, 2, 512), F32),
        in_specs=[pl.BlockSpec(memory_space=pltpu.SMEM)] * 2 + [vmem] * 4,
        out_specs=vmem,
        name="assemble",
    )(at[0], at[2], *[pltpu.with_memory_space_constraint(v, pltpu.VMEM) for v in (*keep, *other)])


def shards(eigvecs, perambulator, time_pairs, momenta):
    zh, zl, y, c = (lax.axis_index(n) for n in ("zh", "zl", "y", "c"))
    slab = (zh * 16 + zl * 8 + y * 2 + c).reshape(1)
    at = (zh.reshape(1), y.reshape(1), c.reshape(1))
    partial, send = elementals(momenta, slab, at[2], eigvecs.reshape(2 * ROWS, NVEC))
    partial = partial + swapped(send, "c")
    partial, perambulator = lax.optimization_barrier((partial, perambulator))
    parts = lax.all_to_all(partial.reshape(16, 2, BLK, NVEC), ("zh", "zl", "y"), 0, 0, tiled=True)
    fold = perambulator[..., :256] + perambulator[..., 256:]
    fold = jnp.transpose(fold, (1, 2, 0, 3))
    mine = lax.dynamic_index_in_dim(fold, c, 0, keepdims=False)
    theirs = lax.dynamic_index_in_dim(fold, 1 - c, 0, keepdims=False)
    sign = jnp.where(zh == 0, 1.0, -1.0)
    cols = jnp.stack([
        sign * (mine - swapped(mine, "zh")),
        sign * (swapped(theirs, "c") - swapped(theirs, ("zh", "c"), 3)),
    ])
    elem = lax.all_to_all(spread(parts), ("x", "zl", "y"), 0, 0, tiled=True).reshape(4, 2, 4, 2, BLK, NVEC)
    cols = [cols] + [swapped(cols, "y", j) for j in (1, 2, 3)]
    elem, cols = lax.optimization_barrier((elem, cols))
    elem = (elem, swapped(elem, "c"))
    keep, send = dress(time_pairs, at, elem, cols)
    keep = [keep, swapped(keep, "zh")]
    send = [send, swapped(send, "zh")]
    return assemble(at, keep, [swapped(v, "c") for v in send])


def solution(mesh):
    fine = Mesh(mesh.devices.reshape(4, 2, 2, 4, 2), ("x", "zh", "zl", "y", "c"))
    slab = ("zh", "zl", "y", "c")
    return jax.shard_map(
        shards,
        mesh=fine,
        in_specs=(P("x", None, slab, None, None), P(slab, "x", None, None), P("x", None), P()),
        out_specs=P(slab, "x", None, None, None),
        check_vma=False,
    )
```

```python
import functools
import math

import jax
import jax.numpy as jnp
from jax import lax
from jax.experimental import pallas as pl
from jax.experimental.pallas import tpu as pltpu
from jax.sharding import Mesh
from jax.sharding import PartitionSpec as P

LS = 48
NMOM = 4
NVEC = 128
NCOL = 3
SITES = 432
ROWS = NCOL * SITES
FULL = 1280
NSITE = 13824
BLK = 16
F32 = jnp.float32
BF16 = jnp.bfloat16


def halves(x):
    hi = x.astype(BF16)
    return hi, (x - hi.astype(F32)).astype(BF16)


def dot(a, b):
    return jnp.dot(a, b, preferred_element_type=F32)


def over48(x):
    return lax.shift_right_logical(x * 43691, 21)


def phase_rows(mom, slab, lanes, first, period):
    lane = lax.broadcasted_iota(jnp.int32, (8, lanes), 1) % period + first
    row = lax.broadcasted_iota(jnp.int32, (8, lanes), 0)
    site = lane - jnp.where(lane >= 2 * SITES, 2 * SITES, jnp.where(lane >= SITES, SITES, 0)) + slab * SITES
    line = over48(site)
    plane = over48(line)
    coords = (site - LS * line, line - LS * plane, plane)
    mrow = row & 3
    turns = jnp.where(row >= 4, 7 * LS - 12, 6 * LS)
    for d in range(3):
        p = jnp.where(mrow == 0, mom[0, d], jnp.where(mrow == 1, mom[1, d], jnp.where(mrow == 2, mom[2, d], mom[3, d])))
        turns = turns + p * coords[d]
    turns = turns - LS * over48(turns)
    return jnp.cos(turns.astype(F32) * (2.0 * math.pi / LS))


def turned(tab, m, at, bt):
    cos, sin = tab[m:m + 1], tab[4 + m:5 + m]
    return jnp.concatenate([cos * at + sin * bt, cos * bt - sin * at], axis=0)


def elemental_kernel(mom, slab, core, x, keep, send):
    tab = phase_rows(mom, slab[0], FULL, 0, FULL)
    tail = phase_rows(mom, slab[0], 3 * BLK, FULL, BLK)
    a = x[pl.ds(2 * FULL, BLK, stride=2), :]
    b = x[pl.ds(2 * FULL + 1, BLK, stride=2), :]
    whi, wlo = halves(jnp.concatenate([a, b], axis=1))
    w = jnp.concatenate([whi, whi, wlo], axis=0)
    at = jnp.concatenate([a, a, a], axis=0).T
    bt = jnp.concatenate([b, b, b], axis=0).T
    lane = lax.broadcasted_iota(jnp.int32, (2 * NVEC, 3 * BLK), 1)
    middle = (lane >= BLK) & (lane < 2 * BLK)
    total = []
    for m in range(NMOM):
        u = turned(tail, m, at, bt)
        hi = u.astype(BF16).astype(F32)
        total.append(dot(jnp.where(middle, u - hi, hi).astype(BF16), w))
    for k0 in range(0, FULL, 256):
        a = x[pl.ds(2 * k0, 256, stride=2), :]
        b = x[pl.ds(2 * k0 + 1, 256, stride=2), :]
        whi, wlo = halves(jnp.concatenate([a, b], axis=1))
        at, bt = a.T, b.T
        for m in range(NMOM):
            hi, lo = halves(turned(tab[:, k0:k0 + 256], m, at, bt))
            total[m] = total[m] + (dot(hi, whi) + dot(lo, whi) + dot(hi, wlo))
    for m in range(NMOM):
        re = total[m][:NVEC, :NVEC] + total[m][NVEC:, NVEC:]
        im = total[m][:NVEC, NVEC:] - total[m][NVEC:, :NVEC]
        for n, part in enumerate((re, im)):
            part = part.reshape(4, 2, BLK, NVEC)
            first, second = part[:, 0], part[:, 1]
            odd = core[0] == 1
            keep[m, :, n] = jnp.where(odd, second, first)
            send[m, :, n] = jnp.where(odd, first, second)


def elementals(mom, slab, core, x):
    return pl.pallas_call(
        elemental_kernel,
        out_shape=[pltpu.VMEM((NMOM, 4, 2, BLK, NVEC), F32)] * 2,
        in_specs=[
            pl.BlockSpec(memory_space=pltpu.SMEM),
            pl.BlockSpec(memory_space=pltpu.SMEM),
            pl.BlockSpec(memory_space=pltpu.SMEM),
            pl.BlockSpec(memory_space=pltpu.VMEM),
        ],
        out_specs=[pl.BlockSpec(memory_space=pltpu.VMEM)] * 2,
        cost_estimate=pl.CostEstimate(flops=10_000_000_000, transcendentals=0, bytes_accessed=20_000_000),
        name="elementals",
    )(mom, slab, core, x)


def times_i(x):
    rows = x.shape[0]
    y = x.reshape(rows // 8, 8, x.shape[1])
    even = lax.broadcasted_iota(jnp.int32, y.shape, 1) % 2 == 0
    y = jnp.where(even, -pltpu.roll(y, 7, 1), pltpu.roll(y, 1, 1))
    return y.reshape(x.shape)


def dress_kernel(tp, yat, cat, mine, theirs, *refs):
    blocks, outs, lrows, cols, rows = refs[:4], refs[4:6], refs[6], refs[7], refs[8]
    elem = (mine, theirs)
    y, c = yat[0], cat[0]
    t1, t2 = tp[c, 0], tp[c, 1]
    for j in range(4):
        for h in range(2):
            cols[2 * (y ^ j) + (c ^ h)] = blocks[j][h]
    rr = cols[...]
    rcat = jnp.concatenate([rr[:, 0].reshape(NVEC, 2 * NVEC), rr[:, 1].reshape(NVEC, 2 * NVEC)], axis=0)
    rhi, rlo = halves(rcat)
    for m in range(2):
        for h in range(2):
            src = elem[h][t1, m, y]
            first = 64 * m + 32 * h
            lrows[pl.ds(first, BLK, stride=2), :] = src[0]
            lrows[pl.ds(first + 1, BLK, stride=2), :] = -src[1]
    left = lrows[...]
    lhi, llo = halves(jnp.concatenate([left, times_i(left)], axis=1))
    t = dot(lhi, rhi) + dot(llo, rhi) + dot(lhi, rlo)
    it = times_i(t)
    for m in range(2):
        for h in range(2):
            for yy in range(4):
                rows[m, 2 * yy + (c ^ h)] = elem[h][t2, m, yy]
        sink = rows[m]
        both = jnp.concatenate([sink[:, 0].reshape(NVEC, NVEC), sink[:, 1].reshape(NVEC, NVEC)], axis=1)
        ehi, elo = halves(both)
        e_both = jnp.concatenate([ehi, elo], axis=0)
        tm, im = t[64 * m:64 * m + 64], it[64 * m:64 * m + 64]
        left = jnp.concatenate(
            [jnp.concatenate([tm[:, l * NVEC:(l + 1) * NVEC], im[:, l * NVEC:(l + 1) * NVEC]], axis=1) for l in range(2)],
            axis=0,
        )
        fhi, flo = halves(left)
        nt = (((1,), (1,)), ((), ()))
        w = lax.dot_general(fhi, e_both, nt, preferred_element_type=F32)
        w = w[:, :NVEC] + w[:, NVEC:] + lax.dot_general(flo, ehi, nt, preferred_element_type=F32)
        for l in range(2):
            for h in range(2):
                outs[h][m, l] = w[64 * l + 32 * h:64 * l + 32 * h + 32]


def dress(tp, at, elem, cols):
    smem = pl.BlockSpec(memory_space=pltpu.SMEM)
    vmem = pl.BlockSpec(memory_space=pltpu.VMEM)
    return pl.pallas_call(
        dress_kernel,
        out_shape=[pltpu.VMEM((2, 2, 2 * BLK, NVEC), F32)] * 2,
        in_specs=[smem, smem, smem] + [vmem] * 6,
        out_specs=[vmem] * 2,
        scratch_shapes=[
            pltpu.VMEM((8 * BLK, NVEC), F32),
            pltpu.VMEM((8, 2, BLK, 2 * NVEC), F32),
            pltpu.VMEM((2, 8, 2, BLK, NVEC), F32),
        ],
        name="dress",
    )(tp, at[1], at[2], *[pltpu.with_memory_space_constraint(v, pltpu.VMEM) for v in (*elem, *cols)])


def spread_kernel(parts, o):
    total = parts[0]
    for n in range(1, 16):
        total = total + parts[n]
    total = total * (1.0 / math.sqrt(2.0 * NCOL * NSITE))
    for n in range(32):
        o[n] = total


def spread(parts):
    vmem = pl.BlockSpec(memory_space=pltpu.VMEM)
    return pl.pallas_call(
        spread_kernel,
        out_shape=pltpu.VMEM((32, 2, BLK, NVEC), F32),
        in_specs=[vmem],
        out_specs=vmem,
        name="spread",
    )(pltpu.with_memory_space_constraint(parts, pltpu.VMEM))


def swapped(x, axis, bits=1):
    size = 2 if axis in ("c", "zh") else 4
    return lax.ppermute(x, axis, [(i, i ^ bits) for i in range(size)])


def assemble_kernel(other_pair, hat, cat, keep, other, *refs):
    out, both, sem = refs[-3:]
    high, c = hat[0], cat[0]
    sign = jnp.where(high == 1, -1.0, 1.0)
    for n, part in enumerate((keep, other)):
        for m in range(2):
            for l in range(2):
                tile = (part[m, l] * sign).reshape(BLK, 2, NVEC)
                for v in range(2):
                    both[:, c ^ n, m, :, 256 * v + NVEC * l:256 * v + NVEC * (l + 1)] = tile
    copy = pltpu.make_async_copy(both, out.at[:, :, pl.ds(2 * (high ^ other_pair), 2)], sem)
    copy.start()
    copy.wait()


def assemble(at, keep, other, done=None):
    smem, vmem = pl.BlockSpec(memory_space=pltpu.SMEM), pl.BlockSpec(memory_space=pltpu.VMEM)
    hbm = pl.BlockSpec(memory_space=pl.ANY)
    second = done is not None
    return pl.pallas_call(
        functools.partial(assemble_kernel, int(second)),
        out_shape=jax.ShapeDtypeStruct((BLK, 2, NMOM, 2, 512), F32),
        in_specs=[smem, smem, vmem, vmem] + [hbm] * second,
        out_specs=hbm,
        scratch_shapes=[pltpu.VMEM((BLK, 2, 2, 2, 512), F32), pltpu.SemaphoreType.DMA],
        input_output_aliases={4: 0} if second else {},
        cost_estimate=pl.CostEstimate(flops=1_000_000_000, transcendentals=0, bytes_accessed=1_000_000),
        name="assemble",
    )(at[0], at[2], *[pltpu.with_memory_space_constraint(v, pltpu.VMEM) for v in (keep, other)], *[done] * second)


def shards(eigvecs, perambulator, time_pairs, momenta):
    zh, zl, y, c = (lax.axis_index(n) for n in ("zh", "zl", "y", "c"))
    slab = (zh * 16 + zl * 8 + y * 2 + c).reshape(1)
    at = (zh.reshape(1), y.reshape(1), c.reshape(1))
    partial, send = elementals(momenta, slab, at[2], eigvecs.reshape(2 * ROWS, NVEC))
    partial = partial + swapped(send, "c")
    partial, perambulator = lax.optimization_barrier((partial, perambulator))
    parts = lax.all_to_all(partial.reshape(16, 2, BLK, NVEC), ("zh", "zl", "y"), 0, 0, tiled=True)
    fold = perambulator[..., :256] + perambulator[..., 256:]
    fold = jnp.transpose(fold, (1, 2, 0, 3))
    mine = lax.dynamic_index_in_dim(fold, c, 0, keepdims=False)
    theirs = lax.dynamic_index_in_dim(fold, 1 - c, 0, keepdims=False)
    sign = jnp.where(zh == 0, 1.0, -1.0)
    cols = jnp.stack([
        sign * (mine - swapped(mine, "zh")),
        sign * (swapped(theirs, "c") - swapped(theirs, ("zh", "c"), 3)),
    ])
    elem = lax.all_to_all(spread(parts), ("x", "zl", "y"), 0, 0, tiled=True).reshape(4, 2, 4, 2, BLK, NVEC)
    cols = [cols] + [swapped(cols, "y", j) for j in (1, 2, 3)]
    elem, cols = lax.optimization_barrier((elem, cols))
    elem = (elem, swapped(elem, "c"))
    keep, send = dress(time_pairs, at, elem, cols)
    far_keep, far_send = swapped(keep, "zh"), swapped(send, "zh")
    half = assemble(at, keep, swapped(send, "c"))
    return assemble(at, far_keep, swapped(far_send, "c"), half)


def solution(mesh):
    fine = Mesh(mesh.devices.reshape(4, 2, 2, 4, 2), ("x", "zh", "zl", "y", "c"))
    slab = ("zh", "zl", "y", "c")
    return jax.shard_map(
        shards,
        mesh=fine,
        in_specs=(P("x", None, slab, None, None), P(slab, "x", None, None), P("x", None), P()),
        out_specs=P(slab, "x", None, None, None),
        check_vma=False,
    )
```

```python
import functools
import math

import jax
import jax.numpy as jnp
from jax import lax
from jax.experimental import pallas as pl
from jax.experimental.pallas import tpu as pltpu
from jax.sharding import Mesh
from jax.sharding import PartitionSpec as P

LS = 48
NMOM = 4
NVEC = 128
NCOL = 3
SITES = 432
ROWS = NCOL * SITES
FULL = 1280
NSITE = 13824
BLK = 16
F32 = jnp.float32
BF16 = jnp.bfloat16


def halves(x):
    hi = x.astype(BF16)
    return hi, (x - hi.astype(F32)).astype(BF16)


def dot(a, b):
    return jnp.dot(a, b, preferred_element_type=F32)


def over48(x):
    return lax.shift_right_logical(x * 43691, 21)


def phase_rows(mom, slab, lanes, first, period):
    lane = lax.broadcasted_iota(jnp.int32, (8, lanes), 1) % period + first
    row = lax.broadcasted_iota(jnp.int32, (8, lanes), 0)
    site = lane - jnp.where(lane >= 2 * SITES, 2 * SITES, jnp.where(lane >= SITES, SITES, 0)) + slab * SITES
    line = over48(site)
    plane = over48(line)
    coords = (site - LS * line, line - LS * plane, plane)
    mrow = row & 3
    turns = jnp.where(row >= 4, 7 * LS - 12, 6 * LS)
    for d in range(3):
        p = jnp.where(mrow == 0, mom[0, d], jnp.where(mrow == 1, mom[1, d], jnp.where(mrow == 2, mom[2, d], mom[3, d])))
        turns = turns + p * coords[d]
    turns = turns - LS * over48(turns)
    return jnp.cos(turns.astype(F32) * (2.0 * math.pi / LS))


def turned(tab, m, at, bt):
    cos, sin = tab[m:m + 1], tab[4 + m:5 + m]
    return jnp.concatenate([cos * at + sin * bt, cos * bt - sin * at], axis=0)


def elemental_kernel(mom, slab, core, x, keep, send):
    tab = phase_rows(mom, slab[0], FULL, 0, FULL)
    tail = phase_rows(mom, slab[0], 3 * BLK, FULL, BLK)
    a = x[pl.ds(2 * FULL, BLK, stride=2), :]
    b = x[pl.ds(2 * FULL + 1, BLK, stride=2), :]
    whi, wlo = halves(jnp.concatenate([a, b], axis=1))
    w = jnp.concatenate([whi, whi, wlo], axis=0)
    at = jnp.concatenate([a, a, a], axis=0).T
    bt = jnp.concatenate([b, b, b], axis=0).T
    lane = lax.broadcasted_iota(jnp.int32, (2 * NVEC, 3 * BLK), 1)
    middle = (lane >= BLK) & (lane < 2 * BLK)
    total = []
    for m in range(NMOM):
        u = turned(tail, m, at, bt)
        hi = u.astype(BF16).astype(F32)
        total.append(dot(jnp.where(middle, u - hi, hi).astype(BF16), w))
    for k0 in range(0, FULL, 256):
        a = x[pl.ds(2 * k0, 256, stride=2), :]
        b = x[pl.ds(2 * k0 + 1, 256, stride=2), :]
        whi, wlo = halves(jnp.concatenate([a, b], axis=1))
        at, bt = a.T, b.T
        for m in range(NMOM):
            hi, lo = halves(turned(tab[:, k0:k0 + 256], m, at, bt))
            total[m] = total[m] + (dot(hi, whi) + dot(lo, whi) + dot(hi, wlo))
    for m in range(NMOM):
        re = total[m][:NVEC, :NVEC] + total[m][NVEC:, NVEC:]
        im = total[m][:NVEC, NVEC:] - total[m][NVEC:, :NVEC]
        for n, part in enumerate((re, im)):
            part = part.reshape(4, 2, BLK, NVEC)
            first, second = part[:, 0], part[:, 1]
            odd = core[0] == 1
            keep[m, :, n] = jnp.where(odd, second, first)
            send[m, :, n] = jnp.where(odd, first, second)


def elementals(mom, slab, core, x):
    return pl.pallas_call(
        elemental_kernel,
        out_shape=[pltpu.VMEM((NMOM, 4, 2, BLK, NVEC), F32)] * 2,
        in_specs=[
            pl.BlockSpec(memory_space=pltpu.SMEM),
            pl.BlockSpec(memory_space=pltpu.SMEM),
            pl.BlockSpec(memory_space=pltpu.SMEM),
            pl.BlockSpec(memory_space=pltpu.VMEM),
        ],
        out_specs=[pl.BlockSpec(memory_space=pltpu.VMEM)] * 2,
        cost_estimate=pl.CostEstimate(flops=10_000_000_000, transcendentals=0, bytes_accessed=20_000_000),
        name="elementals",
    )(mom, slab, core, x)


def times_i(x):
    rows = x.shape[0]
    y = x.reshape(rows // 8, 8, x.shape[1])
    even = lax.broadcasted_iota(jnp.int32, y.shape, 1) % 2 == 0
    y = jnp.where(even, -pltpu.roll(y, 7, 1), pltpu.roll(y, 1, 1))
    return y.reshape(x.shape)


def columns_kernel(yat, cat, *refs):
    blocks, high, low, cols = refs[:4], refs[4], refs[5], refs[6]
    y, c = yat[0], cat[0]
    for j in range(4):
        for h in range(2):
            cols[2 * (y ^ j) + (c ^ h)] = blocks[j][h]
    rr = cols[...]
    for n in range(2):
        rows = slice(NVEC * n, NVEC * (n + 1))
        high[rows], low[rows] = halves(rr[:, n].reshape(NVEC, 2 * NVEC))


def columns(at, cols):
    smem, vmem = pl.BlockSpec(memory_space=pltpu.SMEM), pl.BlockSpec(memory_space=pltpu.VMEM)
    return pl.pallas_call(
        columns_kernel,
        out_shape=[pltpu.VMEM((2 * NVEC, 2 * NVEC), BF16)] * 2,
        in_specs=[smem] * 2 + [vmem] * 4,
        out_specs=[vmem] * 2,
        scratch_shapes=[pltpu.VMEM((8, 2, BLK, 2 * NVEC), F32)],
        cost_estimate=pl.CostEstimate(flops=500_000_000, transcendentals=0, bytes_accessed=500_000),
        name="columns",
    )(at[1], at[2], *[pltpu.with_memory_space_constraint(v, pltpu.VMEM) for v in cols])


def dress_kernel(tp, yat, cat, mine, theirs, high, low, *refs):
    outs, lrows, rows = refs[:2], refs[2], refs[3]
    elem = (mine, theirs)
    y, c = yat[0], cat[0]
    t1, t2 = tp[c, 0], tp[c, 1]
    rhi, rlo = high[...], low[...]
    for m in range(2):
        for h in range(2):
            src = elem[h][y, m, t1]
            first = 64 * m + 32 * h
            lrows[pl.ds(first, BLK, stride=2), :] = src[0]
            lrows[pl.ds(first + 1, BLK, stride=2), :] = -src[1]
    left = lrows[...]
    lhi, llo = halves(jnp.concatenate([left, times_i(left)], axis=1))
    t = dot(lhi, rhi) + dot(llo, rhi) + dot(lhi, rlo)
    it = times_i(t)
    for m in range(2):
        for h in range(2):
            for yy in range(4):
                rows[m, 2 * yy + (c ^ h)] = elem[h][yy, m, t2]
        sink = rows[m]
        both = jnp.concatenate([sink[:, 0].reshape(NVEC, NVEC), sink[:, 1].reshape(NVEC, NVEC)], axis=1)
        ehi, elo = halves(both)
        e_both = jnp.concatenate([ehi, elo], axis=0)
        tm, im = t[64 * m:64 * m + 64], it[64 * m:64 * m + 64]
        left = jnp.concatenate(
            [jnp.concatenate([tm[:, l * NVEC:(l + 1) * NVEC], im[:, l * NVEC:(l + 1) * NVEC]], axis=1) for l in range(2)],
            axis=0,
        )
        fhi, flo = halves(left)
        nt = (((1,), (1,)), ((), ()))
        w = lax.dot_general(fhi, e_both, nt, preferred_element_type=F32)
        w = w[:, :NVEC] + w[:, NVEC:] + lax.dot_general(flo, ehi, nt, preferred_element_type=F32)
        for l in range(2):
            for h in range(2):
                outs[h][m, l] = w[64 * l + 32 * h:64 * l + 32 * h + 32]


def dress(tp, at, elem, cols):
    smem = pl.BlockSpec(memory_space=pltpu.SMEM)
    vmem = pl.BlockSpec(memory_space=pltpu.VMEM)
    return pl.pallas_call(
        dress_kernel,
        out_shape=[pltpu.VMEM((2, 2, 2 * BLK, NVEC), F32)] * 2,
        in_specs=[smem, smem, smem] + [vmem] * 4,
        out_specs=[vmem] * 2,
        scratch_shapes=[
            pltpu.VMEM((8 * BLK, NVEC), F32),
            pltpu.VMEM((2, 8, 2, BLK, NVEC), F32),
        ],
        name="dress",
    )(tp, at[1], at[2], *[pltpu.with_memory_space_constraint(v, pltpu.VMEM) for v in (*elem, *cols)])


def spread_kernel(parts, o):
    total = parts[0]
    for n in range(1, 16):
        total = total + parts[n]
    total = total * (1.0 / math.sqrt(2.0 * NCOL * NSITE))
    for n in range(32):
        o[n] = total


def spread(parts):
    vmem = pl.BlockSpec(memory_space=pltpu.VMEM)
    return pl.pallas_call(
        spread_kernel,
        out_shape=pltpu.VMEM((32, 2, BLK, NVEC), F32),
        in_specs=[vmem],
        out_specs=vmem,
        name="spread",
    )(pltpu.with_memory_space_constraint(parts, pltpu.VMEM))


def swapped(x, axis, bits=1):
    size = 2 if axis in ("c", "zh") else 4
    return lax.ppermute(x, axis, [(i, i ^ bits) for i in range(size)])


def assemble_kernel(other_pair, hat, cat, keep, other, *refs):
    out, both, sem = refs[-3:]
    high, c = hat[0], cat[0]
    sign = jnp.where(high == 1, -1.0, 1.0)
    for n, part in enumerate((keep, other)):
        for m in range(2):
            for l in range(2):
                tile = (part[m, l] * sign).reshape(BLK, 2, NVEC)
                for v in range(2):
                    both[:, c ^ n, m, :, 256 * v + NVEC * l:256 * v + NVEC * (l + 1)] = tile
    copy = pltpu.make_async_copy(both, out.at[:, :, pl.ds(2 * (high ^ other_pair), 2)], sem)
    copy.start()
    copy.wait()


def assemble(at, keep, other, done=None):
    smem, vmem = pl.BlockSpec(memory_space=pltpu.SMEM), pl.BlockSpec(memory_space=pltpu.VMEM)
    hbm = pl.BlockSpec(memory_space=pl.ANY)
    second = done is not None
    return pl.pallas_call(
        functools.partial(assemble_kernel, int(second)),
        out_shape=jax.ShapeDtypeStruct((BLK, 2, NMOM, 2, 512), F32),
        in_specs=[smem, smem, vmem, vmem] + [hbm] * second,
        out_specs=hbm,
        scratch_shapes=[pltpu.VMEM((BLK, 2, 2, 2, 512), F32), pltpu.SemaphoreType.DMA],
        input_output_aliases={4: 0} if second else {},
        cost_estimate=pl.CostEstimate(flops=1_000_000_000, transcendentals=0, bytes_accessed=1_000_000),
        name="assemble",
    )(at[0], at[2], *[pltpu.with_memory_space_constraint(v, pltpu.VMEM) for v in (keep, other)], *[done] * second)


def shards(eigvecs, perambulator, time_pairs, momenta):
    zh, zl, y, c = (lax.axis_index(n) for n in ("zh", "zl", "y", "c"))
    slab = (zh * 16 + zl * 8 + y * 2 + c).reshape(1)
    at = (zh.reshape(1), y.reshape(1), c.reshape(1))
    partial, send = elementals(momenta, slab, at[2], eigvecs.reshape(2 * ROWS, NVEC))
    partial = partial + swapped(send, "c")
    partial, perambulator = lax.optimization_barrier((partial, perambulator))
    parts = lax.all_to_all(partial.reshape(16, 2, BLK, NVEC), ("zh", "zl", "y"), 0, 0, tiled=True)
    fold = perambulator[..., :256] + perambulator[..., 256:]
    fold = jnp.transpose(fold, (1, 2, 0, 3))
    mine = lax.dynamic_index_in_dim(fold, c, 0, keepdims=False)
    theirs = lax.dynamic_index_in_dim(fold, 1 - c, 0, keepdims=False)
    sign = jnp.where(zh == 0, 1.0, -1.0)
    cols = jnp.stack([
        sign * (mine - swapped(mine, "zh")),
        sign * (swapped(theirs, "c") - swapped(theirs, ("zh", "c"), 3)),
    ])
    elem = lax.all_to_all(spread(parts), ("y", "zl", "x"), 0, 0, tiled=True).reshape(4, 2, 4, 2, BLK, NVEC)
    cols = [cols] + [swapped(cols, "y", j) for j in (1, 2, 3)]
    elem, cols = lax.optimization_barrier((elem, cols))
    elem = (elem, swapped(elem, "c"))
    keep, send = dress(time_pairs, at, elem, columns(at, cols))
    far_keep, far_send = swapped(keep, "zh"), swapped(send, "zh")
    half = assemble(at, keep, swapped(send, "c"))
    return assemble(at, far_keep, swapped(far_send, "c"), half)


def solution(mesh):
    fine = Mesh(mesh.devices.reshape(4, 2, 2, 4, 2), ("x", "zh", "zl", "y", "c"))
    slab = ("zh", "zl", "y", "c")
    return jax.shard_map(
        shards,
        mesh=fine,
        in_specs=(P("x", None, slab, None, None), P(slab, "x", None, None), P("x", None), P()),
        out_specs=P(slab, "x", None, None, None),
        check_vma=False,
    )
```
